256 devices in a mesh: rep: 2 (over core), shard: 128 (over x, z, y).
Axes of the slice: x: 4, y: 4, z: 8, core: 2. Of those that a mesh axis runs over, the one named last changes fastest.
Arguments:
- grad: bfloat16 [192, 512, 2048], P(None, 'shard'), may hold values from -6 to 6
- momentum: bfloat16 [192, 512, 2048], P(None, 'shard'), may hold values from -6 to 6
- owners: int32 [2, 128, 2], replicated, may hold values from 0 to 192, as said below
Outputs:
- new_momentum: bfloat16 [192, 512, 2048], P(None, 'shard')
- update: bfloat16 [192, 512, 2048], P(None, 'shard')
The draws below stay inside these ranges and needn't reach their ends.
Inputs may be any that keep to these rules, and one draw needn't show every extreme that they name: `owners`: no matrix index appears twice. In each device's row of 2 slots the entries naming matrices come before the empty ones (value 192). In every draw some device has all 2 slots filled, and some matrices are named by no slot.
All inputs are finite; a program needn't handle non-finite values.
Results may differ from the reference program's by a relative error of at most 0.013.
Values may be sent and summed in bfloat16 or wider, within the bound.
A program may use at most 128 MiB of HBM per device.

```python
import math
import jax
import jax.numpy as jnp
from jax import lax

R = 512
C = 2048
CAP = 2
ITERS = 3
MATS = 192
N_REP = 2
N_SHARD = 128


def draw_owners(key, part):
    first_key, second_key = jax.random.split(jax.random.fold_in(key, 11))
    devices = N_REP * N_SHARD
    heavy = MATS // 8
    single = MATS * 5 // 8
    device_order = jax.random.permutation(first_key, devices)
    ranking = jnp.zeros((devices,), jnp.int32).at[device_order].set(jnp.arange(devices, dtype=jnp.int32))
    counts = jnp.where(ranking < heavy, CAP, jnp.where(ranking < heavy + single, 1, 0)).astype(jnp.int32)
    starts = jnp.cumsum(counts) - counts
    slot_ids = jnp.arange(CAP, dtype=jnp.int32)
    picks = starts[:, None] + slot_ids[None, :]
    alive = slot_ids[None, :] < counts[:, None]
    matrices = jax.random.permutation(second_key, MATS).astype(jnp.int32)
    table = jnp.where(alive, matrices[jnp.clip(picks, 0, MATS - 1)], MATS)
    return table.reshape(N_REP, N_SHARD, CAP).astype(jnp.int32)


def shard_levels(own_key, shape, cuts, low, top_value):
    gain, own = 1.0, jax.random.fold_in(own_key, 6)
    for dim, blocks in cuts:
        draws = jnp.exp(jax.random.uniform(jax.random.fold_in(own, dim), (blocks,), jnp.float32, low / len(cuts), top_value / len(cuts)))
        gain = gain * jnp.repeat(draws, shape[dim] // blocks).reshape([-1 if axis == dim else 1 for axis in range(len(shape))])
    return gain


def normal_values(key, shape, width, reach, shards=(), kind=jnp.bfloat16):
    factor_of = shard_levels(key, shape, shards, -0.22, 0.18) if shards else 1.0
    values = jax.random.normal(key, shape, jnp.float32) * width * factor_of
    return jnp.minimum(jnp.maximum(values, -reach), reach).astype(kind)


def setup_inputs(seed: int = 0) -> dict:
    key_of = jax.random.split(jax.random.key(seed), 4)
    return {
        "grad": normal_values(key_of[0], (MATS, R, C), 1.0, 6.0, ((1, 128),)),
        "momentum": normal_values(key_of[1], (MATS, R, C), 1.0, 6.0, ((1, 128),)),
        "owners": draw_owners(jax.random.fold_in(key_of[3], 71), 0),
    }


coef_a = 3.4445
coef_b = -4.775
coef_c = 2.0315
mom_decay = 0.95

def newton_schulz(matrix):
    whole = matrix.astype(jnp.float32)
    norm_value = jnp.sqrt(jnp.sum(whole * whole))
    current = (whole / (norm_value + 1e-07)).astype(matrix.dtype)
    scaled = None
    for turn_index in range(ITERS):
        gram = lax.dot_general(current, current, (((1,), (1,)), ((), ())), preferred_element_type=jnp.float32).astype(matrix.dtype)
        square = jnp.dot(gram, gram, preferred_element_type=jnp.float32)
        mixer = (coef_b * gram.astype(jnp.float32) + coef_c * square).astype(matrix.dtype)
        result = coef_a * current.astype(jnp.float32) + jnp.dot(mixer, current, preferred_element_type=jnp.float32)
        if turn_index + 1 < ITERS:
            current = result.astype(matrix.dtype)
        else:
            scaled = (0.2 * math.sqrt(max(R, C)) * result).astype(matrix.dtype)
    return scaled

def reference(grad, momentum, owners):
    fresh = mom_decay * momentum.astype(jnp.float32) + grad.astype(jnp.float32)
    new_momentum = fresh.astype(grad.dtype)
    nesterov = (grad.astype(jnp.float32) + mom_decay * fresh).astype(grad.dtype)
    entries = owners.reshape(-1).astype(jnp.int32)
    listed = jnp.zeros((MATS + 1,), jnp.int32).at[entries].add(1)[:MATS] > 0

    def handle(packed):
        matrix, is_listed = packed
        return lax.cond(is_listed, newton_schulz, lambda value: jnp.zeros_like(value), matrix)
    update = lax.map(handle, (nesterov, listed))
    return (new_momentum, update)
```

```python
import math

import jax
import jax.numpy as jnp
from jax import lax
from jax.experimental import pallas as pl
from jax.experimental.pallas import tpu as pltpu
from jax.sharding import PartitionSpec as P

R = 512
C = 2048
ITERS = 3
MATS = 192

NX, NZ, NY = 4, 8, 4
CHIPS = NX * NZ * NY
PER_REP = MATS // 2
LANES = 128
COLS = C // LANES
ROWS = R // CHIPS
QUAD = 4
GROUPS = 8
PER_GROUP = CHIPS // GROUPS

coef_a = 3.4445
coef_b = -4.775
coef_c = 2.0315
mom_decay = 0.95
out_scale = 0.2 * math.sqrt(max(R, C))


def coords(chip):
    return chip // (NZ * NY), (chip // NY) % NZ, chip % NY


def phase(chip, rep):
    x, z, y = coords(chip)
    return (x + z + y + 2 * rep) % NY


def matrix_of(chip, rep):
    return PER_REP * rep + 3 * (chip // NY) + phase(chip, rep) - 1


def owner_of(slot, rep):
    row = slot // 3
    y = (slot % 3 + 1 + 2 * NY - (row // NZ + row % NZ + 2 * rep) % NY) % NY
    return row * NY + y


def offset(k):
    pair = k // NY
    return pair // NZ, (3 * pair) % NZ, k % NY


def dot(a, b, contract_b):
    return lax.dot_general(a, b, (((1,), (contract_b,)), ((), ())), preferred_element_type=jnp.float32)


def tile(row, col):
    return pl.ds(pl.multiple_of(row * 16, 16), 16), slice(col * LANES, (col + 1) * LANES)


def kernel(src, ret, xbuf, ybuf, xs, send1, recv1, send2, recv2, send3, recv3):
    me = lax.axis_index("shard")
    rep = lax.axis_index("rep")
    x, z, y = coords(me)
    mine = matrix_of(me, rep)
    active = phase(me, rep) != 0

    barrier = pltpu.get_barrier_semaphore()

    def greet(k, _):
        pl.semaphore_signal(barrier, 1, device_id={"shard": (me + k) % CHIPS})
        return 0

    lax.fori_loop(1, CHIPS, greet, 0)
    pl.semaphore_signal(barrier, 1, device_id={"rep": 1 - rep})
    pl.semaphore_wait(barrier, CHIPS)

    def spread(slot, _):
        dst = owner_of(slot, rep)
        matrix = PER_REP * rep + slot

        @pl.when(dst != me)
        def _():
            pltpu.make_async_remote_copy(
                src.at[matrix],
                xbuf.at[me // QUAD, :, me % QUAD],
                send1,
                recv1,
                device_id={"shard": dst},
            ).start()

        return 0

    lax.fori_loop(0, PER_REP, spread, 0)

    @pl.when(active)
    def _():
        pltpu.make_async_copy(src.at[mine], xbuf.at[me // QUAD, :, me % QUAD], recv1).start()
        pltpu.make_async_copy(xbuf, xbuf, recv1).wait()

        def gather(row, total):
            for col in range(COLS):
                part = xbuf[row, col].reshape(16, LANES)
                rows, lanes = tile(row, col)
                xs[rows, lanes] = part
                wide = part.astype(jnp.float32)
                total = total + wide * wide
            return total

        total = lax.fori_loop(0, R // 16, gather, jnp.zeros((16, LANES), jnp.float32))
        inverse = 1.0 / (jnp.sqrt(jnp.sum(total)) + 1e-07)
        current = (xs[...].astype(jnp.float32) * inverse).astype(jnp.bfloat16)
        for turn in range(ITERS):
            gram = dot(current, current, 1).astype(jnp.bfloat16)
            mixer = (coef_b * gram.astype(jnp.float32) + coef_c * dot(gram, gram, 0)).astype(jnp.bfloat16)
            result = coef_a * current.astype(jnp.float32) + dot(mixer, current, 0)
            if turn + 1 < ITERS:
                current = result.astype(jnp.bfloat16)
            else:
                xs[...] = (out_scale * result).astype(jnp.bfloat16)

        def scatter(row, _):
            for col in range(COLS):
                rows, lanes = tile(row, col)
                ybuf[row, col] = xs[rows, lanes].reshape(QUAD, ROWS, LANES)
            return 0

        lax.fori_loop(0, R // 16, scatter, 0)

        pltpu.make_async_copy(ybuf.at[me // QUAD, :, me % QUAD], ret.at[mine], recv2.at[0]).start()

        def back(k, _):
            dx, dz, dy = offset(k)
            dst = ((x + dx) % NX * NZ + (z + dz) % NZ) * NY + (y + dy) % NY
            pltpu.make_async_remote_copy(
                ybuf.at[dst // QUAD, :, dst % QUAD],
                ret.at[mine],
                send2,
                recv2.at[k // PER_GROUP],
                device_id={"shard": dst},
            ).start()
            return 0

        lax.fori_loop(1, CHIPS, back, 0)

    def collect(group, _):
        count = PER_GROUP * 3 // NY
        pltpu.make_async_copy(ret.at[pl.ds(0, count)], ret.at[pl.ds(0, count)], recv2.at[group]).wait()

        def forward(j, _):
            dx, dz, dy = offset(group * PER_GROUP + j)
            origin = ((x + NX - dx) % NX * NZ + (z + NZ - dz) % NZ) * NY + (y + NY - dy) % NY

            @pl.when(phase(origin, rep) != 0)
            def _():
                matrix = matrix_of(origin, rep)
                pltpu.make_async_remote_copy(
                    ret.at[matrix], ret.at[matrix], send3, recv3, device_id={"rep": 1 - rep}
                ).start()

            return 0

        lax.fori_loop(0, PER_GROUP, forward, 0)
        return 0

    lax.fori_loop(0, GROUPS, collect, 0)

    half = ret.at[pl.ds(0, PER_REP)]
    pltpu.make_async_copy(half, half, send3).wait()
    pltpu.make_async_copy(half, half, recv3).wait()

    @pl.when(active)
    def _():
        most = ret.at[pl.ds(0, PER_REP - 1)]
        pltpu.make_async_copy(most, most, send1).wait()
        rest = ret.at[pl.ds(0, CHIPS - 1)]
        pltpu.make_async_copy(rest, rest, send2).wait()

    @pl.when(jnp.logical_not(active))
    def _():
        pltpu.make_async_copy(half, half, send1).wait()


def exchange(nesterov):
    return pl.pallas_call(
        kernel,
        out_shape=jax.ShapeDtypeStruct((MATS, COLS, ROWS, LANES), jnp.bfloat16),
        in_specs=[pl.BlockSpec(memory_space=pl.ANY)],
        out_specs=pl.BlockSpec(memory_space=pl.ANY),
        scratch_shapes=[
            pltpu.VMEM((R // 16, COLS, QUAD, ROWS, LANES), jnp.bfloat16),
            pltpu.VMEM((R // 16, COLS, QUAD, ROWS, LANES), jnp.bfloat16),
            pltpu.VMEM((R, C), jnp.bfloat16),
            pltpu.SemaphoreType.DMA(()),
            pltpu.SemaphoreType.DMA(()),
            pltpu.SemaphoreType.DMA(()),
            pltpu.SemaphoreType.DMA((GROUPS,)),
            pltpu.SemaphoreType.DMA(()),
            pltpu.SemaphoreType.DMA(()),
        ],
        name="orthogonalize",
        compiler_params=pltpu.CompilerParams(
            collective_id=0, has_side_effects=True, vmem_limit_bytes=48 * 1024 * 1024
        ),
    )(nesterov)


def body(grad, momentum, owners):
    fresh = mom_decay * momentum.astype(jnp.float32) + grad.astype(jnp.float32)
    new_momentum = fresh.astype(jnp.bfloat16)
    nesterov = (grad.astype(jnp.float32) + mom_decay * fresh).astype(jnp.bfloat16)
    listed = jnp.any(owners.reshape(-1)[None, :] == jnp.arange(MATS, dtype=jnp.int32)[:, None], axis=1)
    blocks = nesterov.reshape(MATS, ROWS, COLS, LANES).transpose(0, 2, 1, 3)
    finished = exchange(blocks).transpose(0, 2, 1, 3).reshape(MATS, ROWS, C)
    update = jnp.where(listed[:, None, None], finished, jnp.zeros_like(finished))
    return (new_momentum, update)


def solution(mesh):
    placed = (P(None, "shard", None), P(None, "shard", None), P())
    return jax.shard_map(
        body,
        mesh=mesh,
        in_specs=placed,
        out_specs=(P(None, "shard", None), P(None, "shard", None)),
        check_vma=False,
    )
```

```python
import math

import jax
import jax.numpy as jnp
from jax import lax
from jax.experimental import pallas as pl
from jax.experimental.pallas import tpu as pltpu
from jax.sharding import PartitionSpec as P

R = 512
C = 2048
ITERS = 3
MATS = 192

NX, NZ, NY = 4, 8, 4
CHIPS = NX * NZ * NY
PER_REP = MATS // 2
LANES = 128
COLS = C // LANES
ROWS = R // CHIPS
QUAD = 4

coef_a = 3.4445
coef_b = -4.775
coef_c = 2.0315
mom_decay = 0.95
out_scale = 0.2 * math.sqrt(max(R, C))


def coords(chip):
    return chip // (NZ * NY), (chip // NY) % NZ, chip % NY


def phase(chip, rep):
    x, z, y = coords(chip)
    return (x + z + y + 2 * rep) % NY


def matrix_of(chip, rep):
    return PER_REP * rep + 3 * (chip // NY) + phase(chip, rep) - 1


def owner_of(slot, rep):
    row = slot // 3
    y = (slot % 3 + 1 + 2 * NY - (row // NZ + row % NZ + 2 * rep) % NY) % NY
    return row * NY + y


def forth(k, chip):
    return 3 * ((13 * (k % 32) + chip // NY) % 32) + k // 32


def back_order(k):
    return (37 * k) % CHIPS


def dot(a, b, contract_b):
    return lax.dot_general(a, b, (((1,), (contract_b,)), ((), ())), preferred_element_type=jnp.float32)


def tile(row, col):
    return pl.ds(pl.multiple_of(row * 16, 16), 16), slice(col * LANES, (col + 1) * LANES)


def kernel(src, ret, xbuf, ybuf, xs, send1, recv1, send2, recv2, send3, recv3):
    me = lax.axis_index("shard")
    rep = lax.axis_index("rep")
    mine = matrix_of(me, rep)
    active = phase(me, rep) != 0

    barrier = pltpu.get_barrier_semaphore()

    def greet(k, _):
        pl.semaphore_signal(barrier, 1, device_id={"shard": (me + k) % CHIPS})
        return 0

    lax.fori_loop(1, CHIPS, greet, 0)
    pl.semaphore_signal(barrier, 1, device_id={"rep": 1 - rep})
    pl.semaphore_wait(barrier, CHIPS)

    def spread(k, _):
        slot = forth(k, me)
        dst = owner_of(slot, rep)
        matrix = PER_REP * rep + slot

        @pl.when(dst != me)
        def _():
            pltpu.make_async_remote_copy(
                src.at[matrix],
                xbuf.at[me // QUAD, :, me % QUAD],
                send1,
                recv1,
                device_id={"shard": dst},
            ).start()

        return 0

    lax.fori_loop(0, PER_REP, spread, 0)

    @pl.when(active)
    def _():
        pltpu.make_async_copy(src.at[mine], xbuf.at[me // QUAD, :, me % QUAD], recv1).start()
        pltpu.make_async_copy(xbuf, xbuf, recv1).wait()

        def gather(row, total):
            for col in range(COLS):
                part = xbuf[row, col].reshape(16, LANES)
                rows, lanes = tile(row, col)
                xs[rows, lanes] = part
                wide = part.astype(jnp.float32)
                total = total + wide * wide
            return total

        total = lax.fori_loop(0, R // 16, gather, jnp.zeros((16, LANES), jnp.float32))
        inverse = 1.0 / (jnp.sqrt(jnp.sum(total)) + 1e-07)
        current = (xs[...].astype(jnp.float32) * inverse).astype(jnp.bfloat16)
        for turn in range(ITERS):
            gram = dot(current, current, 1).astype(jnp.bfloat16)
            mixer = (coef_b * gram.astype(jnp.float32) + coef_c * dot(gram, gram, 0)).astype(jnp.bfloat16)
            result = coef_a * current.astype(jnp.float32) + dot(mixer, current, 0)
            if turn + 1 < ITERS:
                current = result.astype(jnp.bfloat16)
            else:
                xs[...] = (out_scale * result).astype(jnp.bfloat16)

        def scatter(row, _):
            for col in range(COLS):
                rows, lanes = tile(row, col)
                ybuf[row, col] = xs[rows, lanes].reshape(QUAD, ROWS, LANES)
            return 0

        lax.fori_loop(0, R // 16, scatter, 0)

        def back(k, _):
            dst = back_order(k)

            @pl.when(dst != me)
            def _():
                pltpu.make_async_remote_copy(
                    ybuf.at[dst // QUAD, :, dst % QUAD],
                    ret.at[mine],
                    send2,
                    recv2,
                    device_id={"shard": dst},
                ).start()

            return 0

        lax.fori_loop(0, CHIPS, back, 0)
        pltpu.make_async_copy(ybuf.at[me // QUAD, :, me % QUAD], ret.at[mine], recv2).start()

    half = ret.at[pl.ds(PER_REP * rep, PER_REP)]
    pltpu.make_async_copy(half, half, recv2).wait()
    copy = pltpu.make_async_remote_copy(half, half, send3, recv3, device_id={"rep": 1 - rep})
    copy.start()
    copy.wait()

    @pl.when(active)
    def _():
        most = ret.at[pl.ds(0, PER_REP - 1)]
        pltpu.make_async_copy(most, most, send1).wait()
        rest = ret.at[pl.ds(0, CHIPS - 1)]
        pltpu.make_async_copy(rest, rest, send2).wait()

    @pl.when(jnp.logical_not(active))
    def _():
        pltpu.make_async_copy(half, half, send1).wait()


def exchange(nesterov):
    return pl.pallas_call(
        kernel,
        out_shape=jax.ShapeDtypeStruct((MATS, COLS, ROWS, LANES), jnp.bfloat16),
        in_specs=[pl.BlockSpec(memory_space=pl.ANY)],
        out_specs=pl.BlockSpec(memory_space=pl.ANY),
        scratch_shapes=[
            pltpu.VMEM((R // 16, COLS, QUAD, ROWS, LANES), jnp.bfloat16),
            pltpu.VMEM((R // 16, COLS, QUAD, ROWS, LANES), jnp.bfloat16),
            pltpu.VMEM((R, C), jnp.bfloat16),
            pltpu.SemaphoreType.DMA(()),
            pltpu.SemaphoreType.DMA(()),
            pltpu.SemaphoreType.DMA(()),
            pltpu.SemaphoreType.DMA(()),
            pltpu.SemaphoreType.DMA(()),
            pltpu.SemaphoreType.DMA(()),
        ],
        name="orthogonalize",
        compiler_params=pltpu.CompilerParams(
            collective_id=0, has_side_effects=True, vmem_limit_bytes=48 * 1024 * 1024
        ),
    )(nesterov)


def body(grad, momentum, owners):
    fresh = mom_decay * momentum.astype(jnp.float32) + grad.astype(jnp.float32)
    new_momentum = fresh.astype(jnp.bfloat16)
    nesterov = (grad.astype(jnp.float32) + mom_decay * fresh).astype(jnp.bfloat16)
    listed = jnp.any(owners.reshape(-1)[None, :] == jnp.arange(MATS, dtype=jnp.int32)[:, None], axis=1)
    blocks = nesterov.reshape(MATS, ROWS, COLS, LANES).transpose(0, 2, 1, 3)
    finished = exchange(blocks).transpose(0, 2, 1, 3).reshape(MATS, ROWS, C)
    update = jnp.where(listed[:, None, None], finished, jnp.zeros_like(finished))
    return (new_momentum, update)


def solution(mesh):
    placed = (P(None, "shard", None), P(None, "shard", None), P())
    return jax.shard_map(
        body,
        mesh=mesh,
        in_specs=placed,
        out_specs=(P(None, "shard", None), P(None, "shard", None)),
        check_vma=False,
    )
```

```python
import math

import jax
import jax.numpy as jnp
from jax import lax
from jax.experimental import pallas as pl
from jax.experimental.pallas import tpu as pltpu
from jax.sharding import PartitionSpec as P

R = 512
C = 2048
ITERS = 3
MATS = 192

NX, NZ, NY = 4, 8, 4
CHIPS = NX * NZ * NY
LINES = NX * NZ
PER_REP = MATS // 2
THIRDS = 3
LANES = 128
COLS = C // LANES
ROWS = R // CHIPS
QUAD = 16 // ROWS
CHUNKS = 4
CHUNK = PER_REP // CHUNKS

coef_a = 3.4445
coef_b = -4.775
coef_c = 2.0315
mom_decay = 0.95
out_scale = 0.2 * math.sqrt(max(R, C))


def line_phase(line, rep):
    return (line // NZ + line % NZ + 2 * rep) % NY


def phase(chip, rep):
    return (line_phase(chip // NY, rep) + chip % NY) % NY


def owner_of(third, line, rep):
    return line * NY + (third + 1 + NY - line_phase(line, rep)) % NY


def dot(a, b, contract_b):
    return lax.dot_general(a, b, (((1,), (contract_b,)), ((), ())), preferred_element_type=jnp.float32)


def tile(row, col):
    return pl.ds(pl.multiple_of(row * 16, 16), 16), slice(col * LANES, (col + 1) * LANES)


def kernel(
    grad, momentum, owners, fresh_out, update,
    gbuf, mbuf, fbuf, nbuf, xbuf, ybuf, xs,
    load_sem, store_sem, send1, recv1, send2, recv2, send3, recv3,
):
    me = lax.axis_index("shard")
    rep = lax.axis_index("rep")
    turn_of_me = phase(me, rep)
    active = turn_of_me != 0
    mine = PER_REP * rep + LINES * (turn_of_me - 1) + me // NY

    barrier = pltpu.get_barrier_semaphore()

    def load(part):
        first = jnp.where(part < CHUNKS, rep, 1 - rep) * PER_REP + part % CHUNKS * CHUNK
        where = pl.ds(first, CHUNK)
        return (
            pltpu.make_async_copy(grad.at[where], gbuf.at[where], load_sem.at[0, part]),
            pltpu.make_async_copy(momentum.at[where], mbuf.at[where], load_sem.at[1, part]),
        )

    def start_load(part, _):
        for copy in load(part):
            copy.start()
        return 0

    lax.fori_loop(0, 2 * CHUNKS, start_load, 0)

    def greet(k, _):
        pl.semaphore_signal(barrier, 1, device_id={"shard": (me + k) % CHIPS})
        return 0

    lax.fori_loop(1, CHIPS, greet, 0)
    pl.semaphore_signal(barrier, 1, device_id={"rep": 1 - rep})

    def combine(part, own):
        for copy in load(part):
            copy.wait()
        first = (rep if own else 1 - rep) * PER_REP + part % CHUNKS * CHUNK

        def one(i, _):
            for j in range(0, COLS, QUAD):
                g = gbuf[first + i, j : j + QUAD].reshape(16, LANES).astype(jnp.float32)
                m = mbuf[first + i, j : j + QUAD].reshape(16, LANES).astype(jnp.float32)
                fresh = mom_decay * m + g
                fbuf[first + i, j : j + QUAD] = fresh.astype(jnp.bfloat16).reshape(QUAD, ROWS, LANES)
                if own:
                    nesterov = (g + mom_decay * fresh).astype(jnp.bfloat16)
                    nbuf[part * CHUNK + i, j : j + QUAD] = nesterov.reshape(QUAD, ROWS, LANES)
            return 0

        lax.fori_loop(0, CHUNK, one, 0)

    def own_part(part, _):
        combine(part, True)
        return 0

    lax.fori_loop(0, CHUNKS, own_part, 0)
    pl.semaphore_wait(barrier, CHIPS)

    def spread(k, _):
        third = k // LINES
        line = (13 * (k % LINES) + me // NY) % LINES
        dst = owner_of(third, line, rep)

        @pl.when(dst != me)
        def _():
            pltpu.make_async_remote_copy(
                nbuf.at[LINES * third + line],
                xbuf.at[me // QUAD, :, me % QUAD],
                send1,
                recv1,
                device_id={"shard": dst},
            ).start()

        return 0

    lax.fori_loop(0, PER_REP, spread, 0)

    @pl.when(active)
    def _():
        pltpu.make_async_copy(
            nbuf.at[LINES * (turn_of_me - 1) + me // NY], xbuf.at[me // QUAD, :, me % QUAD], recv1
        ).start()

    def other_part(part, _):
        combine(part, False)
        return 0

    lax.fori_loop(CHUNKS, 2 * CHUNKS, other_part, 0)
    store = pltpu.make_async_copy(fbuf, fresh_out, store_sem)
    store.start()

    @pl.when(active)
    def _():
        pltpu.make_async_copy(xbuf, xbuf, recv1).wait()

        def gather(row, total):
            for col in range(COLS):
                part = xbuf[row, col].reshape(16, LANES)
                rows, lanes = tile(row, col)
                xs[rows, lanes] = part
                wide = part.astype(jnp.float32)
                total = total + wide * wide
            return total

        total = lax.fori_loop(0, R // 16, gather, jnp.zeros((16, LANES), jnp.float32))
        inverse = 1.0 / (jnp.sqrt(jnp.sum(total)) + 1e-07)
        current = (xs[...].astype(jnp.float32) * inverse).astype(jnp.bfloat16)
        listed = jnp.sum((owners[...] == mine).astype(jnp.int32)) > 0
        for turn in range(ITERS):
            gram = dot(current, current, 1).astype(jnp.bfloat16)
            mixer = (coef_b * gram.astype(jnp.float32) + coef_c * dot(gram, gram, 0)).astype(jnp.bfloat16)
            result = coef_a * current.astype(jnp.float32) + dot(mixer, current, 0)
            if turn + 1 < ITERS:
                current = result.astype(jnp.bfloat16)
            else:
                xs[...] = jnp.where(listed, out_scale * result, 0.0).astype(jnp.bfloat16)

        def scatter(row, _):
            for col in range(COLS):
                rows, lanes = tile(row, col)
                ybuf[row, col] = xs[rows, lanes].reshape(QUAD, ROWS, LANES)
            return 0

        lax.fori_loop(0, R // 16, scatter, 0)

        def back(k, _):
            dst = (37 * k) % CHIPS

            @pl.when(dst != me)
            def _():
                pltpu.make_async_remote_copy(
                    ybuf.at[dst // QUAD, :, dst % QUAD],
                    update.at[mine],
                    send2,
                    recv2.at[turn_of_me - 1],
                    device_id={"shard": dst},
                ).start()

            return 0

        lax.fori_loop(0, CHIPS, back, 0)
        pltpu.make_async_copy(
            ybuf.at[me // QUAD, :, me % QUAD], update.at[mine], recv2.at[turn_of_me - 1]
        ).start()

    def third_of(part):
        return update.at[pl.ds(PER_REP * rep + LINES * part, LINES)]

    def forward(part, _):
        pltpu.make_async_copy(third_of(part), third_of(part), recv2.at[part]).wait()
        pltpu.make_async_remote_copy(
            third_of(part), third_of(part), send3.at[part], recv3.at[part], device_id={"rep": 1 - rep}
        ).start()
        return 0

    lax.fori_loop(0, THIRDS, forward, 0)

    def finish(part, _):
        pltpu.make_async_copy(third_of(part), third_of(part), send3.at[part]).wait()
        pltpu.make_async_copy(third_of(part), third_of(part), recv3.at[part]).wait()
        return 0

    lax.fori_loop(0, THIRDS, finish, 0)
    store.wait()

    @pl.when(active)
    def _():
        most = nbuf.at[pl.ds(0, PER_REP - 1)]
        pltpu.make_async_copy(most, most, send1).wait()
        rest = update.at[pl.ds(0, CHIPS - 1)]
        pltpu.make_async_copy(rest, rest, send2).wait()

    @pl.when(jnp.logical_not(active))
    def _():
        pltpu.make_async_copy(nbuf, nbuf, send1).wait()


def whole(count):
    return jax.ShapeDtypeStruct((count, COLS, ROWS, LANES), jnp.bfloat16)


def buffer(*shape):
    return pltpu.VMEM(shape, jnp.bfloat16)


def step(grad, momentum, owners):
    dma = pltpu.SemaphoreType.DMA
    anywhere = pl.BlockSpec(memory_space=pl.ANY)
    in_hbm = pl.BlockSpec(memory_space=pltpu.MemorySpace.HBM)
    return pl.pallas_call(
        kernel,
        out_shape=(whole(MATS), whole(MATS)),
        in_specs=[in_hbm, in_hbm, pl.BlockSpec(memory_space=pltpu.VMEM)],
        out_specs=(anywhere, anywhere),
        scratch_shapes=[
            buffer(MATS, COLS, ROWS, LANES),
            buffer(MATS, COLS, ROWS, LANES),
            buffer(MATS, COLS, ROWS, LANES),
            buffer(PER_REP, COLS, ROWS, LANES),
            buffer(R // 16, COLS, QUAD, ROWS, LANES),
            buffer(R // 16, COLS, QUAD, ROWS, LANES),
            buffer(R, C),
            dma((2, 2 * CHUNKS)),
            dma(()),
            dma(()),
            dma(()),
            dma(()),
            dma((THIRDS,)),
            dma((THIRDS,)),
            dma((THIRDS,)),
        ],
        name="muon_step",
        compiler_params=pltpu.CompilerParams(
            collective_id=0, has_side_effects=True, vmem_limit_bytes=40 * 1024 * 1024
        ),
    )(grad, momentum, owners)


def body(grad, momentum, owners):
    def blocks(a):
        return a.reshape(MATS, ROWS, COLS, LANES).transpose(0, 2, 1, 3)

    def rows(a):
        return a.transpose(0, 2, 1, 3).reshape(MATS, ROWS, C)

    new_momentum, update = step(blocks(grad), blocks(momentum), owners.transpose(0, 2, 1))
    return (rows(new_momentum), rows(update))


def solution(mesh):
    placed = (P(None, "shard", None), P(None, "shard", None), P())
    return jax.shard_map(
        body,
        mesh=mesh,
        in_specs=placed,
        out_specs=(P(None, "shard", None), P(None, "shard", None)),
        check_vma=False,
    )
```

```python
import math

import jax
import jax.numpy as jnp
from jax import lax
from jax.experimental import pallas as pl
from jax.experimental.pallas import tpu as pltpu
from jax.sharding import PartitionSpec as P

R = 512
C = 2048
ITERS = 3
MATS = 192

NX, NZ, NY = 4, 8, 4
CHIPS = NX * NZ * NY
LINES = NX * NZ
PER_REP = MATS // 2
THIRDS = 3
LANES = 128
COLS = C // LANES
ROWS = R // CHIPS
QUAD = 16 // ROWS
CHUNKS = 4
CHUNK = PER_REP // CHUNKS

coef_a = 3.4445
coef_b = -4.775
coef_c = 2.0315
mom_decay = 0.95
out_scale = 0.2 * math.sqrt(max(R, C))


def line_phase(line, rep):
    return (line // NZ + line % NZ + 2 * rep) % NY


def phase(chip, rep):
    return (line_phase(chip // NY, rep) + chip % NY) % NY


def owner_of(third, line, rep):
    return line * NY + (third + 1 + NY - line_phase(line, rep)) % NY


def dot(a, b, contract_b):
    return lax.dot_general(a, b, (((1,), (contract_b,)), ((), ())), preferred_element_type=jnp.float32)


def tile(row, col):
    return pl.ds(pl.multiple_of(row * 16, 16), 16), slice(col * LANES, (col + 1) * LANES)


def kernel(
    grad, momentum, owners, fresh_out, update,
    table, gbuf, mbuf, fbuf, nbuf, xbuf, ybuf, xs,
    load_sem, table_sem, store_sem, send1, recv1, send2, recv2, send3, recv3,
):
    me = lax.axis_index("shard")
    rep = lax.axis_index("rep")
    turn_of_me = phase(me, rep)
    active = turn_of_me != 0
    mine = PER_REP * rep + LINES * (turn_of_me - 1) + me // NY

    barrier = pltpu.get_barrier_semaphore()

    def load(part):
        first = jnp.where(part < CHUNKS, rep, 1 - rep) * PER_REP + part % CHUNKS * CHUNK
        where = pl.ds(first, CHUNK)
        return (
            pltpu.make_async_copy(grad.at[where], gbuf.at[where], load_sem.at[0, part]),
            pltpu.make_async_copy(momentum.at[where], mbuf.at[where], load_sem.at[1, part]),
        )

    def start_load(part, _):
        for copy in load(part):
            copy.start()
        return 0

    lax.fori_loop(0, 2 * CHUNKS, start_load, 0)
    table_load = pltpu.make_async_copy(owners, table, table_sem)
    table_load.start()

    def greet(k, _):
        pl.semaphore_signal(barrier, 1, device_id={"shard": (me + k) % CHIPS})
        return 0

    lax.fori_loop(1, CHIPS, greet, 0)
    pl.semaphore_signal(barrier, 1, device_id={"rep": 1 - rep})

    def combine(part, own):
        for copy in load(part):
            copy.wait()
        first = (rep if own else 1 - rep) * PER_REP + part % CHUNKS * CHUNK

        def one(i, _):
            for j in range(0, COLS, QUAD):
                g = gbuf[first + i, j : j + QUAD].reshape(16, LANES).astype(jnp.float32)
                m = mbuf[first + i, j : j + QUAD].reshape(16, LANES).astype(jnp.float32)
                fresh = mom_decay * m + g
                fbuf[first + i, j : j + QUAD] = fresh.astype(jnp.bfloat16).reshape(QUAD, ROWS, LANES)
                if own:
                    nesterov = (g + mom_decay * fresh).astype(jnp.bfloat16)
                    nbuf[part * CHUNK + i, j : j + QUAD] = nesterov.reshape(QUAD, ROWS, LANES)
            return 0

        lax.fori_loop(0, CHUNK, one, 0)

    def own_part(part, _):
        combine(part, True)
        return 0

    lax.fori_loop(0, CHUNKS, own_part, 0)
    pl.semaphore_wait(barrier, CHIPS)

    def spread(k, _):
        third = k // LINES
        line = (13 * (k % LINES) + me // NY) % LINES
        dst = owner_of(third, line, rep)

        @pl.when(dst != me)
        def _():
            pltpu.make_async_remote_copy(
                nbuf.at[LINES * third + line],
                xbuf.at[me // QUAD, :, me % QUAD],
                send1,
                recv1,
                device_id={"shard": dst},
            ).start()

        return 0

    lax.fori_loop(0, PER_REP, spread, 0)

    @pl.when(active)
    def _():
        pltpu.make_async_copy(
            nbuf.at[LINES * (turn_of_me - 1) + me // NY], xbuf.at[me // QUAD, :, me % QUAD], recv1
        ).start()

    def other_part(part, _):
        combine(part, False)
        return 0

    lax.fori_loop(CHUNKS, 2 * CHUNKS, other_part, 0)
    table_load.wait()
    store = pltpu.make_async_copy(fbuf, fresh_out, store_sem)
    store.start()

    @pl.when(active)
    def _():
        pltpu.make_async_copy(xbuf, xbuf, recv1).wait()

        def gather(row, total):
            for col in range(COLS):
                part = xbuf[row, col].reshape(16, LANES)
                rows, lanes = tile(row, col)
                xs[rows, lanes] = part
                wide = part.astype(jnp.float32)
                total = total + wide * wide
            return total

        total = lax.fori_loop(0, R // 16, gather, jnp.zeros((16, LANES), jnp.float32))
        inverse = 1.0 / (jnp.sqrt(jnp.sum(total)) + 1e-07)
        current = (xs[...].astype(jnp.float32) * inverse).astype(jnp.bfloat16)
        listed = jnp.sum((table[...] == mine).astype(jnp.int32)) > 0
        for turn in range(ITERS):
            gram = dot(current, current, 1).astype(jnp.bfloat16)
            mixer = (coef_b * gram.astype(jnp.float32) + coef_c * dot(gram, gram, 0)).astype(jnp.bfloat16)
            result = coef_a * current.astype(jnp.float32) + dot(mixer, current, 0)
            if turn + 1 < ITERS:
                current = result.astype(jnp.bfloat16)
            else:
                xs[...] = jnp.where(listed, out_scale * result, 0.0).astype(jnp.bfloat16)

        def scatter(row, _):
            for col in range(COLS):
                rows, lanes = tile(row, col)
                ybuf[row, col] = xs[rows, lanes].reshape(QUAD, ROWS, LANES)
            return 0

        lax.fori_loop(0, R // 16, scatter, 0)

        def back(k, _):
            x, z, y = me // (NZ * NY), me // NY % NZ, me % NY
            dst = 37 * k % CHIPS

            @pl.when(dst != me)
            def _():
                pltpu.make_async_remote_copy(
                    ybuf.at[dst // QUAD, :, dst % QUAD],
                    update.at[mine],
                    send2,
                    recv2.at[turn_of_me - 1],
                    device_id={"shard": dst},
                ).start()

            return 0

        lax.fori_loop(0, CHIPS, back, 0)
        pltpu.make_async_copy(
            ybuf.at[me // QUAD, :, me % QUAD], update.at[mine], recv2.at[turn_of_me - 1]
        ).start()

    def third_of(part):
        return update.at[pl.ds(PER_REP * rep + LINES * part, LINES)]

    def forward(part, _):
        pltpu.make_async_copy(third_of(part), third_of(part), recv2.at[part]).wait()
        pltpu.make_async_remote_copy(
            third_of(part), third_of(part), send3.at[part], recv3.at[part], device_id={"rep": 1 - rep}
        ).start()
        return 0

    lax.fori_loop(0, THIRDS, forward, 0)

    def finish(part, _):
        pltpu.make_async_copy(third_of(part), third_of(part), send3.at[part]).wait()
        pltpu.make_async_copy(third_of(part), third_of(part), recv3.at[part]).wait()
        return 0

    lax.fori_loop(0, THIRDS, finish, 0)
    store.wait()

    @pl.when(active)
    def _():
        most = nbuf.at[pl.ds(0, PER_REP - 1)]
        pltpu.make_async_copy(most, most, send1).wait()
        rest = update.at[pl.ds(0, CHIPS - 1)]
        pltpu.make_async_copy(rest, rest, send2).wait()

    @pl.when(jnp.logical_not(active))
    def _():
        pltpu.make_async_copy(nbuf, nbuf, send1).wait()


def whole(count):
    return jax.ShapeDtypeStruct((count, COLS, ROWS, LANES), jnp.bfloat16)


def buffer(*shape):
    return pltpu.VMEM(shape, jnp.bfloat16)


def step(grad, momentum, owners):
    dma = pltpu.SemaphoreType.DMA
    anywhere = pl.BlockSpec(memory_space=pl.ANY)
    return pl.pallas_call(
        kernel,
        out_shape=(whole(MATS), whole(MATS)),
        in_specs=[anywhere, anywhere, anywhere],
        out_specs=(anywhere, anywhere),
        scratch_shapes=[
            pltpu.VMEM((2, 2, CHIPS), jnp.int32),
            buffer(MATS, COLS, ROWS, LANES),
            buffer(MATS, COLS, ROWS, LANES),
            buffer(MATS, COLS, ROWS, LANES),
            buffer(PER_REP, COLS, ROWS, LANES),
            buffer(R // 16, COLS, QUAD, ROWS, LANES),
            buffer(R // 16, COLS, QUAD, ROWS, LANES),
            buffer(R, C),
            dma((2, 2 * CHUNKS)),
            dma(()),
            dma(()),
            dma(()),
            dma(()),
            dma(()),
            dma((THIRDS,)),
            dma((THIRDS,)),
            dma((THIRDS,)),
        ],
        name="muon_step",
        compiler_params=pltpu.CompilerParams(
            collective_id=0, has_side_effects=True, vmem_limit_bytes=40 * 1024 * 1024
        ),
    )(grad, momentum, owners)


def body(grad, momentum, owners):
    def in_hbm(a):
        return pltpu.with_memory_space_constraint(a, pltpu.MemorySpace.HBM)

    def blocks(a):
        return a.reshape(MATS, ROWS, COLS, LANES).transpose(0, 2, 1, 3)

    def rows(a):
        return a.transpose(0, 2, 1, 3).reshape(MATS, ROWS, C)

    new_momentum, update = step(in_hbm(blocks(grad)), in_hbm(blocks(momentum)), in_hbm(owners.transpose(0, 2, 1)))
    return (rows(new_momentum), rows(update))


def solution(mesh):
    placed = (P(None, "shard", None), P(None, "shard", None), P())
    return jax.shard_map(
        body,
        mesh=mesh,
        in_specs=placed,
        out_specs=(P(None, "shard", None), P(None, "shard", None)),
        check_vma=False,
    )
```

```python
import functools
import math

import jax
import jax.numpy as jnp
from jax import lax
from jax.experimental import pallas as pl
from jax.experimental.pallas import tpu as pltpu
from jax.sharding import PartitionSpec as P

R = 512
C = 2048
ITERS = 3
MATS = 192

NX, NZ, NY = 4, 8, 4
CHIPS = NX * NZ * NY
PER_REP = MATS // 2
THIRDS = 3
LANES = 128
COLS = C // LANES
ROWS = R // CHIPS
QUAD = 16 // ROWS
CHUNKS = 4
CHUNK = PER_REP // CHUNKS

coef_a = 3.4445
coef_b = -4.775
coef_c = 2.0315
mom_decay = 0.95
out_scale = 0.2 * math.sqrt(max(R, C))


def line_phase(line, rep):
    return (line // NZ + line % NZ + 2 * rep) % NY


def phase(chip, rep):
    return (line_phase(chip // NY, rep) + chip % NY) % NY


def first_z(x, third, rep):
    return x + 4 * rep


def place_in_third(line, third, rep, depth):
    x, z = line // NZ, line % NZ
    rank = (z + 8 * NZ - first_z(x, third, rep)) % NZ
    return jnp.where(rank < depth, x * depth + rank, NX * NZ)


def owner_of(third, place, rep, depth):
    x = place // depth
    line = x * NZ + (place % depth + first_z(x, third, rep)) % NZ
    return line * NY + (third + 1 + NY - line_phase(line, rep)) % NY


def dot(a, b, contract_b):
    return lax.dot_general(a, b, (((1,), (contract_b,)), ((), ())), preferred_element_type=jnp.float32)


def tile(row, col):
    return pl.ds(pl.multiple_of(row * 16, 16), 16), slice(col * LANES, (col + 1) * LANES)


def kernel(
    depth, order, grad, momentum, fresh_out, update,
    gbuf, mbuf, fbuf, nbuf, xbuf, ybuf, xs,
    load_sem, store_sem, send1, recv1, send2, recv2, send3, recv3,
):
    me = lax.axis_index("shard")
    rep = lax.axis_index("rep")
    lines = NX * depth
    used = THIRDS * lines
    turn_of_me = phase(me, rep)
    my_third = (turn_of_me + NY - 1) % NY
    my_place = place_in_third(me // NY, my_third, rep, depth)
    active = jnp.logical_and(turn_of_me != 0, my_place < lines)
    my_slot = lines * my_third + my_place
    mine = PER_REP * rep + my_slot

    barrier = pltpu.get_barrier_semaphore()

    def load(part):
        where = pl.ds(part * CHUNK, CHUNK)
        return (
            pltpu.make_async_copy(grad.at[where], gbuf.at[where], load_sem.at[0, part]),
            pltpu.make_async_copy(momentum.at[where], mbuf.at[where], load_sem.at[1, part]),
        )

    def start_load(part, _):
        for copy in load(part):
            copy.start()
        return 0

    lax.fori_loop(0, 2 * CHUNKS, start_load, 0)

    def greet(k, _):
        pl.semaphore_signal(barrier, 1, device_id={"shard": (me + k) % CHIPS})
        return 0

    lax.fori_loop(1, CHIPS, greet, 0)
    pl.semaphore_signal(barrier, 1, device_id={"rep": 1 - rep})

    def end_load(part, _):
        for copy in load(part):
            copy.wait()
        return 0

    lax.fori_loop(0, 2 * CHUNKS, end_load, 0)

    def fresh_of(matrix, j):
        g = gbuf[matrix, j : j + QUAD].reshape(16, LANES).astype(jnp.float32)
        m = mbuf[matrix, j : j + QUAD].reshape(16, LANES).astype(jnp.float32)
        return g, mom_decay * m + g

    def look_ahead(slot, _):
        matrix = order[PER_REP * rep + slot]
        for j in range(0, COLS, QUAD):
            g, fresh = fresh_of(matrix, j)
            nesterov = (g + mom_decay * fresh).astype(jnp.bfloat16)
            nbuf[slot, j : j + QUAD] = nesterov.reshape(QUAD, ROWS, LANES)
        return 0

    lax.fori_loop(0, used, look_ahead, 0)
    pl.semaphore_wait(barrier, CHIPS)

    def spread(k, _):
        third = k // lines
        place = (13 * (k % lines) + me // NY) % lines
        dst = owner_of(third, place, rep, depth)

        @pl.when(dst != me)
        def _():
            pltpu.make_async_remote_copy(
                nbuf.at[lines * third + place],
                xbuf.at[me // QUAD, :, me % QUAD],
                send1,
                recv1,
                device_id={"shard": dst},
            ).start()

        return 0

    lax.fori_loop(0, used, spread, 0)

    @pl.when(active)
    def _():
        pltpu.make_async_copy(
            nbuf.at[my_slot], xbuf.at[me // QUAD, :, me % QUAD], recv1
        ).start()

    def renew(matrix, _):
        for j in range(0, COLS, QUAD):
            fresh = fresh_of(matrix, j)[1]
            fbuf[matrix, j : j + QUAD] = fresh.astype(jnp.bfloat16).reshape(QUAD, ROWS, LANES)
        return 0

    lax.fori_loop(0, MATS, renew, 0)
    store = pltpu.make_async_copy(fbuf, fresh_out, store_sem)
    store.start()

    @pl.when(active)
    def _():
        pltpu.make_async_copy(xbuf, xbuf, recv1).wait()

        def gather(row, total):
            for col in range(COLS):
                part = xbuf[row, col].reshape(16, LANES)
                rows, lanes = tile(row, col)
                xs[rows, lanes] = part
                wide = part.astype(jnp.float32)
                total = total + wide * wide
            return total

        total = lax.fori_loop(0, R // 16, gather, jnp.zeros((16, LANES), jnp.float32))
        inverse = 1.0 / (jnp.sqrt(jnp.sum(total)) + 1e-07)
        current = (xs[...].astype(jnp.float32) * inverse).astype(jnp.bfloat16)
        for turn in range(ITERS):
            gram = dot(current, current, 1).astype(jnp.bfloat16)
            mixer = (coef_b * gram.astype(jnp.float32) + coef_c * dot(gram, gram, 0)).astype(jnp.bfloat16)
            result = coef_a * current.astype(jnp.float32) + dot(mixer, current, 0)
            if turn + 1 < ITERS:
                current = result.astype(jnp.bfloat16)
            else:
                xs[...] = (out_scale * result).astype(jnp.bfloat16)

        def scatter(row, _):
            for col in range(COLS):
                rows, lanes = tile(row, col)
                ybuf[row, col] = xs[rows, lanes].reshape(QUAD, ROWS, LANES)
            return 0

        lax.fori_loop(0, R // 16, scatter, 0)

        def back(k, _):
            x, z, y = me // (NZ * NY), me // NY % NZ, me % NY
            dst = 37 * k % CHIPS

            @pl.when(dst != me)
            def _():
                pltpu.make_async_remote_copy(
                    ybuf.at[dst // QUAD, :, dst % QUAD],
                    update.at[mine],
                    send2,
                    recv2.at[my_third],
                    device_id={"shard": dst},
                ).start()

            return 0

        lax.fori_loop(0, CHIPS, back, 0)
        pltpu.make_async_copy(
            ybuf.at[me // QUAD, :, me % QUAD], update.at[mine], recv2.at[my_third]
        ).start()

    def third_of(part):
        return update.at[pl.ds(PER_REP * rep + lines * part, lines)]

    def forward(part, _):
        pltpu.make_async_copy(third_of(part), third_of(part), recv2.at[part]).wait()
        pltpu.make_async_remote_copy(
            third_of(part), third_of(part), send3.at[part], recv3.at[part], device_id={"rep": 1 - rep}
        ).start()
        return 0

    lax.fori_loop(0, THIRDS, forward, 0)

    def finish(part, _):
        pltpu.make_async_copy(third_of(part), third_of(part), send3.at[part]).wait()
        pltpu.make_async_copy(third_of(part), third_of(part), recv3.at[part]).wait()
        return 0

    lax.fori_loop(0, THIRDS, finish, 0)
    store.wait()

    @pl.when(active)
    def _():
        most = nbuf.at[pl.ds(0, used - 1)]
        pltpu.make_async_copy(most, most, send1).wait()
        rest = update.at[pl.ds(0, CHIPS - 1)]
        pltpu.make_async_copy(rest, rest, send2).wait()

    @pl.when(jnp.logical_not(active))
    def _():
        full = nbuf.at[pl.ds(0, used)]
        pltpu.make_async_copy(full, full, send1).wait()


def whole(count):
    return jax.ShapeDtypeStruct((count, COLS, ROWS, LANES), jnp.bfloat16)


def buffer(*shape):
    return pltpu.VMEM(shape, jnp.bfloat16)


def put_out(where, fresh, packed, fresh_out, update, zeros, sem):
    zeros[...] = jnp.zeros_like(zeros)
    pltpu.make_async_copy(fresh, fresh_out, sem.at[0]).start()

    def one(matrix, _):
        slot = where[matrix]

        @pl.when(slot >= 0)
        def _():
            pltpu.make_async_copy(packed.at[jnp.maximum(slot, 0)], update.at[matrix], sem.at[1]).start()

        @pl.when(slot < 0)
        def _():
            pltpu.make_async_copy(zeros, update.at[matrix], sem.at[1]).start()

        return 0

    lax.fori_loop(0, MATS, one, 0)
    pltpu.make_async_copy(fresh, fresh_out, sem.at[0]).wait()
    pltpu.make_async_copy(fresh, update, sem.at[1]).wait()


def step(depth, grad, momentum, order, where):
    dma = pltpu.SemaphoreType.DMA
    anywhere = pl.BlockSpec(memory_space=pl.ANY)
    scalars = pl.BlockSpec(memory_space=pltpu.SMEM)
    fresh, packed = pl.pallas_call(
        functools.partial(kernel, depth),
        out_shape=(whole(MATS), whole(MATS)),
        in_specs=[scalars, anywhere, anywhere],
        out_specs=(anywhere, anywhere),
        scratch_shapes=[
            buffer(MATS, COLS, ROWS, LANES),
            buffer(MATS, COLS, ROWS, LANES),
            buffer(MATS, COLS, ROWS, LANES),
            buffer(PER_REP, COLS, ROWS, LANES),
            buffer(R // 16, COLS, QUAD, ROWS, LANES),
            buffer(R // 16, COLS, QUAD, ROWS, LANES),
            buffer(R, C),
            dma((2, 2 * CHUNKS)),
            dma(()),
            dma(()),
            dma(()),
            dma(()),
            dma((THIRDS,)),
            dma((THIRDS,)),
            dma((THIRDS,)),
        ],
        name=f"muon_step_{depth}",
        compiler_params=pltpu.CompilerParams(
            collective_id=depth, has_side_effects=True, vmem_limit_bytes=40 * 1024 * 1024
        ),
    )(order, grad, momentum)
    return pl.pallas_call(
        put_out,
        out_shape=(whole(MATS), whole(MATS)),
        in_specs=[scalars, anywhere, anywhere],
        out_specs=(anywhere, anywhere),
        scratch_shapes=[buffer(COLS, ROWS, LANES), dma((2,))],
        name=f"put_out_{depth}",
        compiler_params=pltpu.CompilerParams(vmem_limit_bytes=1024 * 1024),
    )(where, fresh, packed)


DEPTHS = (7, NZ)


def body(grad, momentum, owners):
    def in_hbm(a):
        return pltpu.with_memory_space_constraint(a, pltpu.MemorySpace.HBM)

    def blocks(a):
        return in_hbm(a.reshape(MATS, ROWS, COLS, LANES).transpose(0, 2, 1, 3))

    def rows(a):
        return a.transpose(0, 2, 1, 3).reshape(MATS, ROWS, C)

    index = jnp.arange(MATS, dtype=jnp.int32)
    table = owners.transpose(0, 2, 1).reshape(4, CHIPS)
    listed = jnp.any(table[:, :, None] == index, axis=(0, 1))
    before = jnp.sum((listed[:, None] & (index[:, None] < index[None, :])).astype(jnp.int32), axis=0)
    few = jnp.sum(listed.astype(jnp.int32)) <= 2 * THIRDS * NX * DEPTHS[0]
    used = jnp.where(few, THIRDS * NX * DEPTHS[0], PER_REP)
    where = jnp.where(listed, jnp.where(before < used, before, PER_REP + before - used), -1)
    order = jnp.sum(jnp.where(where[:, None] == index[None, :], index[:, None], 0), axis=0)
    new_momentum, update = lax.cond(
        few,
        functools.partial(step, DEPTHS[0]),
        functools.partial(step, DEPTHS[1]),
        blocks(grad), blocks(momentum), order, where,
    )
    return (rows(new_momentum), rows(update))


def solution(mesh):
    placed = (P(None, "shard", None), P(None, "shard", None), P())
    return jax.shard_map(
        body,
        mesh=mesh,
        in_specs=placed,
        out_specs=(P(None, "shard", None), P(None, "shard", None)),
        check_vma=False,
    )
```

```python
import functools
import math

import jax
import jax.numpy as jnp
from jax import lax
from jax.experimental import pallas as pl
from jax.experimental.pallas import tpu as pltpu
from jax.sharding import PartitionSpec as P

R = 512
C = 2048
ITERS = 3
MATS = 192

NX, NZ, NY = 4, 8, 4
CHIPS = NX * NZ * NY
PER_REP = MATS // 2
THIRDS = 3
LANES = 128
COLS = C // LANES
ROWS = R // CHIPS
QUAD = 16 // ROWS
CHUNKS = 4
CHUNK = PER_REP // CHUNKS

coef_a = 3.4445
coef_b = -4.775
coef_c = 2.0315
mom_decay = 0.95
out_scale = 0.2 * math.sqrt(max(R, C))


def line_phase(line, rep):
    return (line // NZ + line % NZ + 2 * rep) % NY


def phase(chip, rep):
    return (line_phase(chip // NY, rep) + chip % NY) % NY


def first_z(x, third, rep):
    return x + 4 * rep


def place_in_third(line, third, rep, depth):
    x, z = line // NZ, line % NZ
    rank = (z + 8 * NZ - first_z(x, third, rep)) % NZ
    return jnp.where(rank < depth, x * depth + rank, NX * NZ)


def owner_of(third, place, rep, depth):
    x = place // depth
    line = x * NZ + (place % depth + first_z(x, third, rep)) % NZ
    return line * NY + (third + 1 + NY - line_phase(line, rep)) % NY


def hops(chip):
    at = (chip // (NZ * NY), chip // NY % NZ, chip % NY)
    return sum(min(a, n - a) for a, n in zip(at, (NX, NZ, NY)))


NEAR_FIRST = sorted((37 * k % CHIPS for k in range(CHIPS)), key=hops)


def dot(a, b, contract_b):
    return lax.dot_general(a, b, (((1,), (contract_b,)), ((), ())), preferred_element_type=jnp.float32)


def tile(row, col):
    return pl.ds(pl.multiple_of(row * 16, 16), 16), slice(col * LANES, (col + 1) * LANES)


def kernel(
    depth, order, grad, momentum, fresh_out, update,
    gbuf, mbuf, fbuf, nbuf, xbuf, ybuf, xs,
    load_sem, store_sem, send1, recv1, send2, recv2, send3, recv3,
):
    me = lax.axis_index("shard")
    rep = lax.axis_index("rep")
    lines = NX * depth
    used = THIRDS * lines
    turn_of_me = phase(me, rep)
    my_third = (turn_of_me + NY - 1) % NY
    my_place = place_in_third(me // NY, my_third, rep, depth)
    active = jnp.logical_and(turn_of_me != 0, my_place < lines)
    my_slot = lines * my_third + my_place
    mine = PER_REP * rep + my_slot

    barrier = pltpu.get_barrier_semaphore()

    def load(part):
        where = pl.ds(part * CHUNK, CHUNK)
        return (
            pltpu.make_async_copy(grad.at[where], gbuf.at[where], load_sem.at[0, part]),
            pltpu.make_async_copy(momentum.at[where], mbuf.at[where], load_sem.at[1, part]),
        )

    def start_load(part, _):
        for copy in load(part):
            copy.start()
        return 0

    lax.fori_loop(0, 2 * CHUNKS, start_load, 0)

    def greet(k, _):
        pl.semaphore_signal(barrier, 1, device_id={"shard": (me + k) % CHIPS})
        return 0

    lax.fori_loop(1, CHIPS, greet, 0)
    pl.semaphore_signal(barrier, 1, device_id={"rep": 1 - rep})

    def end_load(part, _):
        for copy in load(part):
            copy.wait()
        return 0

    lax.fori_loop(0, 2 * CHUNKS, end_load, 0)

    def fresh_of(matrix, j):
        g = gbuf[matrix, j : j + QUAD].reshape(16, LANES).astype(jnp.float32)
        m = mbuf[matrix, j : j + QUAD].reshape(16, LANES).astype(jnp.float32)
        return g, mom_decay * m + g

    def look_ahead(slot, _):
        matrix = order[PER_REP * rep + slot]
        for j in range(0, COLS, QUAD):
            g, fresh = fresh_of(matrix, j)
            nesterov = (g + mom_decay * fresh).astype(jnp.bfloat16)
            nbuf[slot, j : j + QUAD] = nesterov.reshape(QUAD, ROWS, LANES)
        return 0

    lax.fori_loop(0, used, look_ahead, 0)
    pl.semaphore_wait(barrier, CHIPS)

    def spread(k, _):
        third = k // lines
        place = (13 * (k % lines) + me // NY) % lines
        dst = owner_of(third, place, rep, depth)

        @pl.when(dst != me)
        def _():
            pltpu.make_async_remote_copy(
                nbuf.at[lines * third + place],
                xbuf.at[me // QUAD, :, me % QUAD],
                send1,
                recv1,
                device_id={"shard": dst},
            ).start()

        return 0

    lax.fori_loop(0, used, spread, 0)

    @pl.when(active)
    def _():
        pltpu.make_async_copy(
            nbuf.at[my_slot], xbuf.at[me // QUAD, :, me % QUAD], recv1
        ).start()

    def renew(matrix, _):
        for j in range(0, COLS, QUAD):
            fresh = fresh_of(matrix, j)[1]
            fbuf[matrix, j : j + QUAD] = fresh.astype(jnp.bfloat16).reshape(QUAD, ROWS, LANES)
        return 0

    lax.fori_loop(0, MATS, renew, 0)
    store = pltpu.make_async_copy(fbuf, fresh_out, store_sem)
    store.start()

    @pl.when(active)
    def _():
        pltpu.make_async_copy(xbuf, xbuf, recv1).wait()

        def gather(row, total):
            for col in range(COLS):
                part = xbuf[row, col].reshape(16, LANES)
                rows, lanes = tile(row, col)
                xs[rows, lanes] = part
                wide = part.astype(jnp.float32)
                total = total + wide * wide
            return total

        total = lax.fori_loop(0, R // 16, gather, jnp.zeros((16, LANES), jnp.float32))
        inverse = 1.0 / (jnp.sqrt(jnp.sum(total)) + 1e-07)
        current = (xs[...].astype(jnp.float32) * inverse).astype(jnp.bfloat16)
        for turn in range(ITERS):
            gram = dot(current, current, 1).astype(jnp.bfloat16)
            mixer = (coef_b * gram.astype(jnp.float32) + coef_c * dot(gram, gram, 0)).astype(jnp.bfloat16)
            result = coef_a * current.astype(jnp.float32) + dot(mixer, current, 0)
            if turn + 1 < ITERS:
                current = result.astype(jnp.bfloat16)
            else:
                xs[...] = (out_scale * result).astype(jnp.bfloat16)

        def scatter(row, _):
            for col in range(COLS):
                rows, lanes = tile(row, col)
                ybuf[row, col] = xs[rows, lanes].reshape(QUAD, ROWS, LANES)
            return 0

        lax.fori_loop(0, R // 16, scatter, 0)

        def back(dst):
            @pl.when(dst != me)
            def _():
                pltpu.make_async_remote_copy(
                    ybuf.at[dst // QUAD, :, dst % QUAD],
                    update.at[mine],
                    send2,
                    recv2.at[my_third],
                    device_id={"shard": dst},
                ).start()

        for dst in NEAR_FIRST:
            back(dst)

        pltpu.make_async_copy(
            ybuf.at[me // QUAD, :, me % QUAD], update.at[mine], recv2.at[my_third]
        ).start()

    def third_of(part):
        return update.at[pl.ds(PER_REP * rep + lines * part, lines)]

    def forward(part, _):
        pltpu.make_async_copy(third_of(part), third_of(part), recv2.at[part]).wait()
        pltpu.make_async_remote_copy(
            third_of(part), third_of(part), send3.at[part], recv3.at[part], device_id={"rep": 1 - rep}
        ).start()
        return 0

    lax.fori_loop(0, THIRDS, forward, 0)

    def finish(part, _):
        pltpu.make_async_copy(third_of(part), third_of(part), send3.at[part]).wait()
        pltpu.make_async_copy(third_of(part), third_of(part), recv3.at[part]).wait()
        return 0

    lax.fori_loop(0, THIRDS, finish, 0)
    store.wait()

    @pl.when(active)
    def _():
        most = nbuf.at[pl.ds(0, used - 1)]
        pltpu.make_async_copy(most, most, send1).wait()
        rest = update.at[pl.ds(0, CHIPS - 1)]
        pltpu.make_async_copy(rest, rest, send2).wait()

    @pl.when(jnp.logical_not(active))
    def _():
        full = nbuf.at[pl.ds(0, used)]
        pltpu.make_async_copy(full, full, send1).wait()


def whole(count):
    return jax.ShapeDtypeStruct((count, COLS, ROWS, LANES), jnp.bfloat16)


def buffer(*shape):
    return pltpu.VMEM(shape, jnp.bfloat16)


def put_out(where, fresh, packed, fresh_out, update, zeros, sem):
    zeros[...] = jnp.zeros_like(zeros)
    pltpu.make_async_copy(fresh, fresh_out, sem.at[0]).start()

    def one(matrix, _):
        slot = where[matrix]

        @pl.when(slot >= 0)
        def _():
            pltpu.make_async_copy(packed.at[jnp.maximum(slot, 0)], update.at[matrix], sem.at[1]).start()

        @pl.when(slot < 0)
        def _():
            pltpu.make_async_copy(zeros, update.at[matrix], sem.at[1]).start()

        return 0

    lax.fori_loop(0, MATS, one, 0)
    pltpu.make_async_copy(fresh, fresh_out, sem.at[0]).wait()
    pltpu.make_async_copy(fresh, update, sem.at[1]).wait()


def step(depth, grad, momentum, order, where):
    dma = pltpu.SemaphoreType.DMA
    anywhere = pl.BlockSpec(memory_space=pl.ANY)
    scalars = pl.BlockSpec(memory_space=pltpu.SMEM)
    fresh, packed = pl.pallas_call(
        functools.partial(kernel, depth),
        out_shape=(whole(MATS), whole(MATS)),
        in_specs=[scalars, anywhere, anywhere],
        out_specs=(anywhere, anywhere),
        scratch_shapes=[
            buffer(MATS, COLS, ROWS, LANES),
            buffer(MATS, COLS, ROWS, LANES),
            buffer(MATS, COLS, ROWS, LANES),
            buffer(PER_REP, COLS, ROWS, LANES),
            buffer(R // 16, COLS, QUAD, ROWS, LANES),
            buffer(R // 16, COLS, QUAD, ROWS, LANES),
            buffer(R, C),
            dma((2, 2 * CHUNKS)),
            dma(()),
            dma(()),
            dma(()),
            dma(()),
            dma((THIRDS,)),
            dma((THIRDS,)),
            dma((THIRDS,)),
        ],
        name=f"muon_step_{depth}",
        compiler_params=pltpu.CompilerParams(
            collective_id=depth, has_side_effects=True, vmem_limit_bytes=40 * 1024 * 1024
        ),
    )(order, grad, momentum)
    return pl.pallas_call(
        put_out,
        out_shape=(whole(MATS), whole(MATS)),
        in_specs=[scalars, anywhere, anywhere],
        out_specs=(anywhere, anywhere),
        scratch_shapes=[buffer(COLS, ROWS, LANES), dma((2,))],
        name=f"put_out_{depth}",
        compiler_params=pltpu.CompilerParams(vmem_limit_bytes=1024 * 1024),
    )(where, fresh, packed)


DEPTHS = (7, NZ)


def body(grad, momentum, owners):
    def in_hbm(a):
        return pltpu.with_memory_space_constraint(a, pltpu.MemorySpace.HBM)

    def blocks(a):
        return in_hbm(a.reshape(MATS, ROWS, COLS, LANES).transpose(0, 2, 1, 3))

    def rows(a):
        return a.transpose(0, 2, 1, 3).reshape(MATS, ROWS, C)

    index = jnp.arange(MATS, dtype=jnp.int32)
    table = owners.transpose(0, 2, 1).reshape(4, CHIPS)
    listed = jnp.any(table[:, :, None] == index, axis=(0, 1))
    before = jnp.sum((listed[:, None] & (index[:, None] < index[None, :])).astype(jnp.int32), axis=0)
    few = jnp.sum(listed.astype(jnp.int32)) <= 2 * THIRDS * NX * DEPTHS[0]
    used = jnp.where(few, THIRDS * NX * DEPTHS[0], PER_REP)
    where = jnp.where(listed, jnp.where(before < used, before, PER_REP + before - used), -1)
    order = jnp.sum(jnp.where(where[:, None] == index[None, :], index[:, None], 0), axis=0)
    new_momentum, update = lax.cond(
        few,
        functools.partial(step, DEPTHS[0]),
        functools.partial(step, DEPTHS[1]),
        blocks(grad), blocks(momentum), order, where,
    )
    return (rows(new_momentum), rows(update))


def solution(mesh):
    placed = (P(None, "shard", None), P(None, "shard", None), P())
    return jax.shard_map(
        body,
        mesh=mesh,
        in_specs=placed,
        out_specs=(P(None, "shard", None), P(None, "shard", None)),
        check_vma=False,
    )
```

```python
import functools
import math

import jax
import jax.numpy as jnp
from jax import lax
from jax.experimental import pallas as pl
from jax.experimental.pallas import tpu as pltpu
from jax.sharding import PartitionSpec as P

R = 512
C = 2048
ITERS = 3
MATS = 192

NX, NZ, NY = 4, 8, 4
CHIPS = NX * NZ * NY
PER_REP = MATS // 2
THIRDS = 3
LANES = 128
COLS = C // LANES
ROWS = R // CHIPS
QUAD = 16 // ROWS
CHUNKS = 4
CHUNK = PER_REP // CHUNKS

coef_a = 3.4445
coef_b = -4.775
coef_c = 2.0315
mom_decay = 0.95
out_scale = 0.2 * math.sqrt(max(R, C))


def line_phase(line, rep):
    return (line // NZ + line % NZ + 2 * rep) % NY


def phase(chip, rep):
    return (line_phase(chip // NY, rep) + chip % NY) % NY


def first_z(x, third, rep):
    return x + 4 * rep


def place_in_third(line, third, rep, depth):
    x, z = line // NZ, line % NZ
    rank = (z + 8 * NZ - first_z(x, third, rep)) % NZ
    return jnp.where(rank < depth, x * depth + rank, NX * NZ)


def owner_of(third, place, rep, depth):
    x = place // depth
    line = x * NZ + (place % depth + first_z(x, third, rep)) % NZ
    return line * NY + (third + 1 + NY - line_phase(line, rep)) % NY


def hops(chip):
    at = (chip // (NZ * NY), chip // NY % NZ, chip % NY)
    return sum(min(a, n - a) for a, n in zip(at, (NX, NZ, NY)))


NEAR_FIRST = sorted((37 * k % CHIPS for k in range(CHIPS)), key=hops)


def dot(a, b, contract_b):
    return lax.dot_general(a, b, (((1,), (contract_b,)), ((), ())), preferred_element_type=jnp.float32)


def tile(row, col):
    return pl.ds(pl.multiple_of(row * 16, 16), 16), slice(col * LANES, (col + 1) * LANES)


def kernel(
    depth, order, grad, momentum, fresh_out, update,
    gbuf, mbuf, fbuf, nbuf, xbuf, ybuf, xs,
    load_sem, store_sem, send1, recv1, send2, recv2, send3, recv3,
):
    me = lax.axis_index("shard")
    rep = lax.axis_index("rep")
    lines = NX * depth
    used = THIRDS * lines
    turn_of_me = phase(me, rep)
    my_third = (turn_of_me + NY - 1) % NY
    my_place = place_in_third(me // NY, my_third, rep, depth)
    active = jnp.logical_and(turn_of_me != 0, my_place < lines)
    my_slot = lines * my_third + my_place
    mine = PER_REP * rep + my_slot

    barrier = pltpu.get_barrier_semaphore()

    def load(part):
        where = pl.ds(part * CHUNK, CHUNK)
        return (
            pltpu.make_async_copy(grad.at[where], gbuf.at[where], load_sem.at[0, part]),
            pltpu.make_async_copy(momentum.at[where], mbuf.at[where], load_sem.at[1, part]),
        )

    def start_load(part, _):
        for copy in load(part):
            copy.start()
        return 0

    lax.fori_loop(0, 2 * CHUNKS, start_load, 0)

    def greet(k, _):
        pl.semaphore_signal(barrier, 1, device_id={"shard": (me + k) % CHIPS})
        return 0

    lax.fori_loop(1, CHIPS, greet, 0)
    pl.semaphore_signal(barrier, 1, device_id={"rep": 1 - rep})

    def end_load(part, _):
        for copy in load(part):
            copy.wait()
        return 0

    lax.fori_loop(0, 2 * CHUNKS, end_load, 0)

    def fresh_of(matrix, j):
        g = gbuf[matrix, j : j + QUAD].reshape(16, LANES).astype(jnp.float32)
        m = mbuf[matrix, j : j + QUAD].reshape(16, LANES).astype(jnp.float32)
        return g, mom_decay * m + g

    def look_ahead(slot, _):
        matrix = order[PER_REP * rep + slot]
        for j in range(0, COLS, QUAD):
            g, fresh = fresh_of(matrix, j)
            nesterov = (g + mom_decay * fresh).astype(jnp.bfloat16)
            nbuf[slot, j : j + QUAD] = nesterov.reshape(QUAD, ROWS, LANES)
        return 0

    lax.fori_loop(0, used, look_ahead, 0)
    pl.semaphore_wait(barrier, CHIPS)

    def spread(k, _):
        third = k // lines
        place = (13 * (k % lines) + me // NY) % lines
        dst = owner_of(third, place, rep, depth)

        @pl.when(dst != me)
        def _():
            pltpu.make_async_remote_copy(
                nbuf.at[lines * third + place],
                xbuf.at[me // QUAD, :, me % QUAD],
                send1,
                recv1,
                device_id={"shard": dst},
            ).start()

        return 0

    lax.fori_loop(0, used, spread, 0)

    @pl.when(active)
    def _():
        pltpu.make_async_copy(
            nbuf.at[my_slot], xbuf.at[me // QUAD, :, me % QUAD], recv1
        ).start()

    def renew(matrix, _):
        for j in range(0, COLS, QUAD):
            fresh = fresh_of(matrix, j)[1]
            fbuf[matrix, j : j + QUAD] = fresh.astype(jnp.bfloat16).reshape(QUAD, ROWS, LANES)
        return 0

    lax.fori_loop(0, MATS, renew, 0)
    store = pltpu.make_async_copy(fbuf, fresh_out, store_sem)
    store.start()

    @pl.when(active)
    def _():
        pltpu.make_async_copy(xbuf, xbuf, recv1).wait()

        def gather(row, total):
            for col in range(COLS):
                part = xbuf[row, col].reshape(16, LANES)
                rows, lanes = tile(row, col)
                xs[rows, lanes] = part
                wide = part.astype(jnp.float32)
                total = total + wide * wide
            return total

        total = lax.fori_loop(0, R // 16, gather, jnp.zeros((16, LANES), jnp.float32))
        inverse = 1.0 / (jnp.sqrt(jnp.sum(total)) + 1e-07)
        current = (xs[...].astype(jnp.float32) * inverse).astype(jnp.bfloat16)
        for turn in range(ITERS):
            gram = dot(current, current, 1).astype(jnp.bfloat16)
            mixer = (coef_b * gram.astype(jnp.float32) + coef_c * dot(gram, gram, 0)).astype(jnp.bfloat16)
            result = coef_a * current.astype(jnp.float32) + dot(mixer, current, 0)
            if turn + 1 < ITERS:
                current = result.astype(jnp.bfloat16)
            else:
                xs[...] = (out_scale * result).astype(jnp.bfloat16)

        def scatter(row, _):
            for col in range(COLS):
                rows, lanes = tile(row, col)
                ybuf[row, col] = xs[rows, lanes].reshape(QUAD, ROWS, LANES)
            return 0

        lax.fori_loop(0, R // 16, scatter, 0)

        def back(dst):
            @pl.when(dst != me)
            def _():
                pltpu.make_async_remote_copy(
                    ybuf.at[dst // QUAD, :, dst % QUAD],
                    update.at[mine],
                    send2,
                    recv2.at[my_third],
                    device_id={"shard": dst},
                ).start()

        for dst in NEAR_FIRST:
            back(dst)

        pltpu.make_async_copy(
            ybuf.at[me // QUAD, :, me % QUAD], update.at[mine], recv2.at[my_third]
        ).start()

    def third_of(part):
        return update.at[pl.ds(PER_REP * rep + lines * part, lines)]

    def forward(part, _):
        pltpu.make_async_copy(third_of(part), third_of(part), recv2.at[part]).wait()
        pltpu.make_async_remote_copy(
            third_of(part), third_of(part), send3.at[part], recv3.at[part], device_id={"rep": 1 - rep}
        ).start()
        return 0

    lax.fori_loop(0, THIRDS, forward, 0)

    def finish(part, _):
        pltpu.make_async_copy(third_of(part), third_of(part), send3.at[part]).wait()
        pltpu.make_async_copy(third_of(part), third_of(part), recv3.at[part]).wait()
        return 0

    lax.fori_loop(0, THIRDS, finish, 0)
    store.wait()

    @pl.when(active)
    def _():
        most = nbuf.at[pl.ds(0, used - 1)]
        pltpu.make_async_copy(most, most, send1).wait()
        rest = update.at[pl.ds(0, CHIPS - 1)]
        pltpu.make_async_copy(rest, rest, send2).wait()

    @pl.when(jnp.logical_not(active))
    def _():
        full = nbuf.at[pl.ds(0, used)]
        pltpu.make_async_copy(full, full, send1).wait()


def whole(count):
    return jax.ShapeDtypeStruct((count, COLS, ROWS, LANES), jnp.bfloat16)


def buffer(*shape):
    return pltpu.VMEM(shape, jnp.bfloat16)


def put_out(where, fresh, packed, fresh_out, update, zeros, sem):
    zeros[...] = jnp.zeros_like(zeros)
    pltpu.make_async_copy(fresh, fresh_out, sem.at[0]).start()

    def one(matrix, _):
        slot = where[matrix]

        @pl.when(slot >= 0)
        def _():
            pltpu.make_async_copy(packed.at[jnp.maximum(slot, 0)], update.at[matrix], sem.at[1]).start()

        @pl.when(slot < 0)
        def _():
            pltpu.make_async_copy(zeros, update.at[matrix], sem.at[1]).start()

        return 0

    lax.fori_loop(0, MATS, one, 0)
    pltpu.make_async_copy(fresh, fresh_out, sem.at[0]).wait()
    pltpu.make_async_copy(fresh, update, sem.at[1]).wait()


def step(depth, grad, momentum, order, where):
    dma = pltpu.SemaphoreType.DMA
    anywhere = pl.BlockSpec(memory_space=pl.ANY)
    scalars = pl.BlockSpec(memory_space=pltpu.SMEM)
    fresh, packed = pl.pallas_call(
        functools.partial(kernel, depth),
        out_shape=(whole(MATS), whole(MATS)),
        in_specs=[scalars, anywhere, anywhere],
        out_specs=(anywhere, anywhere),
        scratch_shapes=[
            buffer(MATS, COLS, ROWS, LANES),
            buffer(MATS, COLS, ROWS, LANES),
            buffer(MATS, COLS, ROWS, LANES),
            buffer(PER_REP, COLS, ROWS, LANES),
            buffer(R // 16, COLS, QUAD, ROWS, LANES),
            buffer(R // 16, COLS, QUAD, ROWS, LANES),
            buffer(R, C),
            dma((2, 2 * CHUNKS)),
            dma(()),
            dma(()),
            dma(()),
            dma(()),
            dma((THIRDS,)),
            dma((THIRDS,)),
            dma((THIRDS,)),
        ],
        name=f"muon_step_{depth}",
        compiler_params=pltpu.CompilerParams(
            collective_id=depth, has_side_effects=True, vmem_limit_bytes=40 * 1024 * 1024
        ),
    )(order, grad, momentum)
    return pl.pallas_call(
        put_out,
        out_shape=(whole(MATS), whole(MATS)),
        in_specs=[scalars, anywhere, anywhere],
        out_specs=(anywhere, anywhere),
        scratch_shapes=[buffer(COLS, ROWS, LANES), dma((2,))],
        name=f"put_out_{depth}",
        compiler_params=pltpu.CompilerParams(vmem_limit_bytes=1024 * 1024),
    )(where, fresh, packed)


DEPTHS = (7, NZ)


def body(grad, momentum, owners):
    def in_hbm(a):
        return pltpu.with_memory_space_constraint(a, pltpu.MemorySpace.HBM)

    def blocks(a):
        return in_hbm(a.reshape(MATS, ROWS, COLS, LANES).transpose(0, 2, 1, 3))

    def rows(a):
        return a.transpose(0, 2, 1, 3).reshape(MATS, ROWS, C)

    index = jnp.arange(MATS, dtype=jnp.int32)
    table = owners.transpose(0, 2, 1).reshape(4, CHIPS)
    listed = jnp.any(table[:, :, None] == index, axis=(0, 1))
    before = jnp.sum((listed[:, None] & (index[:, None] < index[None, :])).astype(jnp.int32), axis=0)
    few = jnp.sum((table < MATS).astype(jnp.int32)) <= 2 * THIRDS * NX * DEPTHS[0]
    used = jnp.where(few, THIRDS * NX * DEPTHS[0], PER_REP)
    where = jnp.where(listed, jnp.where(before < used, before, PER_REP + before - used), -1)
    order = jnp.sum(jnp.where(where[:, None] == index[None, :], index[:, None], 0), axis=0)
    new_momentum, update = lax.cond(
        few,
        functools.partial(step, DEPTHS[0]),
        functools.partial(step, DEPTHS[1]),
        blocks(grad), blocks(momentum), order, where,
    )
    return (rows(new_momentum), rows(update))


def solution(mesh):
    placed = (P(None, "shard", None), P(None, "shard", None), P())
    return jax.shard_map(
        body,
        mesh=mesh,
        in_specs=placed,
        out_specs=(P(None, "shard", None), P(None, "shard", None)),
        check_vma=False,
    )
```

```python
import functools
import math

import jax
import jax.numpy as jnp
from jax import lax
from jax.experimental import pallas as pl
from jax.experimental.pallas import tpu as pltpu
from jax.sharding import PartitionSpec as P

R = 512
C = 2048
ITERS = 3
MATS = 192

NX, NZ, NY = 4, 8, 4
CHIPS = NX * NZ * NY
PER_REP = MATS // 2
THIRDS = 3
LANES = 128
COLS = C // LANES
ROWS = R // CHIPS
QUAD = 16 // ROWS
CHUNKS = 4
CHUNK = PER_REP // CHUNKS

coef_a = 3.4445
coef_b = -4.775
coef_c = 2.0315
mom_decay = 0.95
out_scale = 0.2 * math.sqrt(max(R, C))


def line_phase(line, rep):
    return (line // NZ + line % NZ + 2 * rep) % NY


def phase(chip, rep):
    return (line_phase(chip // NY, rep) + chip % NY) % NY


def first_z(x, third, rep):
    return x + 4 * rep


def place_in_third(line, third, rep, depth):
    x, z = line // NZ, line % NZ
    rank = (z + 8 * NZ - first_z(x, third, rep)) % NZ
    return jnp.where(rank < depth, x * depth + rank, NX * NZ)


def owner_of(third, place, rep, depth):
    x = place // depth
    line = x * NZ + (place % depth + first_z(x, third, rep)) % NZ
    return line * NY + (third + 1 + NY - line_phase(line, rep)) % NY


def hops(chip):
    at = (chip // (NZ * NY), chip // NY % NZ, chip % NY)
    return sum(min(a, n - a) for a, n in zip(at, (NX, NZ, NY)))


NEAR_FIRST = sorted((37 * k % CHIPS for k in range(CHIPS)), key=hops)


def dot(a, b, contract_b):
    return lax.dot_general(a, b, (((1,), (contract_b,)), ((), ())), preferred_element_type=jnp.float32)


def tile(row, col):
    return pl.ds(pl.multiple_of(row * 16, 16), 16), slice(col * LANES, (col + 1) * LANES)


def kernel(
    depth, order, grad, momentum, fresh_out, update,
    gbuf, mbuf, fbuf, nbuf, xbuf, ybuf, xs,
    load_sem, store_sem, send1, recv1, send2, recv2, send3, recv3,
):
    me = lax.axis_index("shard")
    rep = lax.axis_index("rep")
    lines = NX * depth
    used = THIRDS * lines
    turn_of_me = phase(me, rep)
    my_third = (turn_of_me + NY - 1) % NY
    my_place = place_in_third(me // NY, my_third, rep, depth)
    active = jnp.logical_and(turn_of_me != 0, my_place < lines)
    my_slot = lines * my_third + my_place
    mine = PER_REP * rep + my_slot

    barrier = pltpu.get_barrier_semaphore()

    def load(part):
        where = pl.ds(part * CHUNK, CHUNK)
        return (
            pltpu.make_async_copy(grad.at[where], gbuf.at[where], load_sem.at[0, part]),
            pltpu.make_async_copy(momentum.at[where], mbuf.at[where], load_sem.at[1, part]),
        )

    def start_load(part, _):
        for copy in load(part):
            copy.start()
        return 0


    def greet(k, _):
        pl.semaphore_signal(barrier, 1, device_id={"shard": (me + k) % CHIPS})
        return 0

    lax.fori_loop(1, CHIPS, greet, 0)
    pl.semaphore_signal(barrier, 1, device_id={"rep": 1 - rep})
    lax.fori_loop(0, 2 * CHUNKS, start_load, 0)

    def end_load(part, _):
        for copy in load(part):
            copy.wait()
        return 0

    lax.fori_loop(0, 2 * CHUNKS, end_load, 0)

    def fresh_of(matrix, j):
        g = gbuf[matrix, j : j + QUAD].reshape(16, LANES).astype(jnp.float32)
        m = mbuf[matrix, j : j + QUAD].reshape(16, LANES).astype(jnp.float32)
        return g, mom_decay * m + g

    def look_ahead(slot, _):
        matrix = order[PER_REP * rep + slot]
        for j in range(0, COLS, QUAD):
            g, fresh = fresh_of(matrix, j)
            nesterov = (g + mom_decay * fresh).astype(jnp.bfloat16)
            nbuf[slot, j : j + QUAD] = nesterov.reshape(QUAD, ROWS, LANES)
        return 0

    lax.fori_loop(0, used, look_ahead, 0)
    pl.semaphore_wait(barrier, CHIPS)

    def spread(k, _):
        third = k // lines
        place = (13 * (k % lines) + me // NY) % lines
        dst = owner_of(third, place, rep, depth)

        @pl.when(dst != me)
        def _():
            pltpu.make_async_remote_copy(
                nbuf.at[lines * third + place],
                xbuf.at[me // QUAD, :, me % QUAD],
                send1,
                recv1,
                device_id={"shard": dst},
            ).start()

        return 0

    lax.fori_loop(0, used, spread, 0)

    @pl.when(active)
    def _():
        pltpu.make_async_copy(
            nbuf.at[my_slot], xbuf.at[me // QUAD, :, me % QUAD], recv1
        ).start()

    def renew(matrix, _):
        for j in range(0, COLS, QUAD):
            fresh = fresh_of(matrix, j)[1]
            fbuf[matrix, j : j + QUAD] = fresh.astype(jnp.bfloat16).reshape(QUAD, ROWS, LANES)
        return 0

    lax.fori_loop(0, MATS, renew, 0)
    store = pltpu.make_async_copy(fbuf, fresh_out, store_sem)
    store.start()

    @pl.when(active)
    def _():
        pltpu.make_async_copy(xbuf, xbuf, recv1).wait()

        def gather(row, total):
            for col in range(COLS):
                part = xbuf[row, col].reshape(16, LANES)
                rows, lanes = tile(row, col)
                xs[rows, lanes] = part
                wide = part.astype(jnp.float32)
                total = total + wide * wide
            return total

        total = lax.fori_loop(0, R // 16, gather, jnp.zeros((16, LANES), jnp.float32))
        inverse = 1.0 / (jnp.sqrt(jnp.sum(total)) + 1e-07)
        current = (xs[...].astype(jnp.float32) * inverse).astype(jnp.bfloat16)
        for turn in range(ITERS):
            gram = dot(current, current, 1).astype(jnp.bfloat16)
            mixer = (coef_b * gram.astype(jnp.float32) + coef_c * dot(gram, gram, 0)).astype(jnp.bfloat16)
            result = coef_a * current.astype(jnp.float32) + dot(mixer, current, 0)
            if turn + 1 < ITERS:
                current = result.astype(jnp.bfloat16)
            else:
                xs[...] = (out_scale * result).astype(jnp.bfloat16)

        def scatter(row, _):
            for col in range(COLS):
                rows, lanes = tile(row, col)
                ybuf[row, col] = xs[rows, lanes].reshape(QUAD, ROWS, LANES)
            return 0

        lax.fori_loop(0, R // 16, scatter, 0)

        def back(dst):
            @pl.when(dst != me)
            def _():
                pltpu.make_async_remote_copy(
                    ybuf.at[dst // QUAD, :, dst % QUAD],
                    update.at[mine],
                    send2,
                    recv2.at[my_third],
                    device_id={"shard": dst},
                ).start()

        for dst in NEAR_FIRST:
            back(dst)

        pltpu.make_async_copy(
            ybuf.at[me // QUAD, :, me % QUAD], update.at[mine], recv2.at[my_third]
        ).start()

    def third_of(part):
        return update.at[pl.ds(PER_REP * rep + lines * part, lines)]

    def forward(part, _):
        pltpu.make_async_copy(third_of(part), third_of(part), recv2.at[part]).wait()
        pltpu.make_async_remote_copy(
            third_of(part), third_of(part), send3.at[part], recv3.at[part], device_id={"rep": 1 - rep}
        ).start()
        return 0

    lax.fori_loop(0, THIRDS, forward, 0)

    def finish(part, _):
        pltpu.make_async_copy(third_of(part), third_of(part), send3.at[part]).wait()
        pltpu.make_async_copy(third_of(part), third_of(part), recv3.at[part]).wait()
        return 0

    lax.fori_loop(0, THIRDS, finish, 0)
    store.wait()

    @pl.when(active)
    def _():
        most = nbuf.at[pl.ds(0, used - 1)]
        pltpu.make_async_copy(most, most, send1).wait()
        rest = update.at[pl.ds(0, CHIPS - 1)]
        pltpu.make_async_copy(rest, rest, send2).wait()

    @pl.when(jnp.logical_not(active))
    def _():
        full = nbuf.at[pl.ds(0, used)]
        pltpu.make_async_copy(full, full, send1).wait()


def whole(count):
    return jax.ShapeDtypeStruct((count, COLS, ROWS, LANES), jnp.bfloat16)


def buffer(*shape):
    return pltpu.VMEM(shape, jnp.bfloat16)


def put_out(where, fresh, packed, fresh_out, update, zeros, sem):
    zeros[...] = jnp.zeros_like(zeros)
    pltpu.make_async_copy(fresh, fresh_out, sem.at[0]).start()

    def one(matrix, _):
        slot = where[matrix]

        @pl.when(slot >= 0)
        def _():
            pltpu.make_async_copy(packed.at[jnp.maximum(slot, 0)], update.at[matrix], sem.at[1]).start()

        @pl.when(slot < 0)
        def _():
            pltpu.make_async_copy(zeros, update.at[matrix], sem.at[1]).start()

        return 0

    lax.fori_loop(0, MATS, one, 0)
    pltpu.make_async_copy(fresh, fresh_out, sem.at[0]).wait()
    pltpu.make_async_copy(fresh, update, sem.at[1]).wait()


def step(depth, grad, momentum, order, where):
    dma = pltpu.SemaphoreType.DMA
    anywhere = pl.BlockSpec(memory_space=pl.ANY)
    scalars = pl.BlockSpec(memory_space=pltpu.SMEM)
    fresh, packed = pl.pallas_call(
        functools.partial(kernel, depth),
        out_shape=(whole(MATS), whole(MATS)),
        in_specs=[scalars, anywhere, anywhere],
        out_specs=(anywhere, anywhere),
        scratch_shapes=[
            buffer(MATS, COLS, ROWS, LANES),
            buffer(MATS, COLS, ROWS, LANES),
            buffer(MATS, COLS, ROWS, LANES),
            buffer(PER_REP, COLS, ROWS, LANES),
            buffer(R // 16, COLS, QUAD, ROWS, LANES),
            buffer(R // 16, COLS, QUAD, ROWS, LANES),
            buffer(R, C),
            dma((2, 2 * CHUNKS)),
            dma(()),
            dma(()),
            dma(()),
            dma(()),
            dma((THIRDS,)),
            dma((THIRDS,)),
            dma((THIRDS,)),
        ],
        name=f"muon_step_{depth}",
        compiler_params=pltpu.CompilerParams(
            collective_id=depth, has_side_effects=True, vmem_limit_bytes=40 * 1024 * 1024
        ),
    )(order, grad, momentum)
    return pl.pallas_call(
        put_out,
        out_shape=(whole(MATS), whole(MATS)),
        in_specs=[scalars, anywhere, anywhere],
        out_specs=(anywhere, anywhere),
        scratch_shapes=[buffer(COLS, ROWS, LANES), dma((2,))],
        name=f"put_out_{depth}",
        compiler_params=pltpu.CompilerParams(vmem_limit_bytes=1024 * 1024),
    )(where, fresh, packed)


DEPTHS = (7, NZ)


def body(grad, momentum, owners):
    def in_hbm(a):
        return pltpu.with_memory_space_constraint(a, pltpu.MemorySpace.HBM)

    def blocks(a):
        return in_hbm(a.reshape(MATS, ROWS, COLS, LANES).transpose(0, 2, 1, 3))

    def rows(a):
        return a.transpose(0, 2, 1, 3).reshape(MATS, ROWS, C)

    index = jnp.arange(MATS, dtype=jnp.int32)
    table = owners.transpose(0, 2, 1).reshape(4, CHIPS)
    listed = jnp.any(table[:, :, None] == index, axis=(0, 1))
    before = jnp.sum((listed[:, None] & (index[:, None] < index[None, :])).astype(jnp.int32), axis=0)
    few = jnp.sum(listed.astype(jnp.int32)) <= 2 * THIRDS * NX * DEPTHS[0]
    used = jnp.where(few, THIRDS * NX * DEPTHS[0], PER_REP)
    where = jnp.where(listed, jnp.where(before < used, before, PER_REP + before - used), -1)
    order = jnp.sum(jnp.where(where[:, None] == index[None, :], index[:, None], 0), axis=0)
    new_momentum, update = lax.cond(
        few,
        functools.partial(step, DEPTHS[0]),
        functools.partial(step, DEPTHS[1]),
        blocks(grad), blocks(momentum), order, where,
    )
    return (rows(new_momentum), rows(update))


def solution(mesh):
    placed = (P(None, "shard", None), P(None, "shard", None), P())
    return jax.shard_map(
        body,
        mesh=mesh,
        in_specs=placed,
        out_specs=(P(None, "shard", None), P(None, "shard", None)),
        check_vma=False,
    )
```
